512 devices in a mesh: inline: 32 (over z, core), xline: 16 (over x, y).
Axes of the slice: x: 4, y: 4, z: 16, core: 2. Of those that a mesh axis runs over, the one named last changes fastest.
Arguments:
- probes: float32 [2, 512, 512, 128], P(None, 'inline', 'xline'), may hold values from -6 to 6
- diffusion: bfloat16 [3, 512, 512, 128], P(None, 'inline', 'xline'), may hold values from -1 to 1, as said below
- wavelet: float32 [41], replicated, may hold values from -1 to 1
Outputs:
- iterate: float32 [2, 512, 512, 128], P(None, 'inline', 'xline')
The draws below stay inside these ranges and needn't reach their ends.
Inputs may be any that keep to these rules, and one draw needn't show every extreme that they name: `diffusion`: components 0 and 2 are positive; component 1 lies within nine tenths of the root of their product in magnitude.
All inputs are finite; a program needn't handle non-finite values.
Results may differ from the reference program's by a relative error of at most 0.0003.
Values may be sent and summed in bfloat16 or wider, within the bound.
No kernel may reach another device: no remote copies, remote signals or barrier semaphores. Data moves between devices by JAX's collectives and lax.ppermute only.
A program may use at most 64 MiB of HBM per device.

```python
import jax
import jax.numpy as jnp
from jax import lax

NT = 128
HALF = 20
TAPS = 41
PAIRS = 3
NV = 2
NI = 512
NX = 512


def draw_diffusion(key, part):
    first_key, second_key, third_key = jax.random.split(jax.random.fold_in(key, 17), 3)
    shape = (NI, NX, NT)
    lower, upper = (0.05, 0.5)
    span_low = jnp.log(jnp.float32(lower))
    span_high = jnp.log(jnp.float32(upper))
    coef_in = jnp.exp(jax.random.uniform(first_key, shape, jnp.float32, span_low, span_high))
    coef_x = jnp.exp(jax.random.uniform(second_key, shape, jnp.float32, span_low, span_high))
    shear = jax.random.uniform(third_key, shape, jnp.float32, -0.9, 0.9)
    coef_mix = shear * jnp.sqrt(coef_in * coef_x)
    return jnp.stack([coef_in, coef_mix, coef_x]).astype(jnp.bfloat16)


def level_of(stream_key, dims, shards, smallest, largest):
    level = 1.0
    for dim, parts in shards:
        steps = jax.random.uniform(jax.random.fold_in(jax.random.fold_in(stream_key, 6), dim), (parts,), jnp.float32, smallest / len(shards), largest / len(shards))
        level = level * jnp.repeat(jnp.exp(steps), dims[dim] // parts).reshape((-1,) + (1,) * (len(dims) - 1 - dim))
    return level


def noise(key, shape, scale, limit, cuts=(), dtype=jnp.bfloat16):
    result = jax.random.normal(key, shape, jnp.float32) * scale
    if len(cuts) > 0:
        result = level_of(key, shape, cuts, -0.22, 0.18) * result
    return jnp.clip(result, min=-limit, max=limit).astype(dtype)


def setup_inputs(seed: int = 0) -> dict:
    seeds = jax.random.split(jax.random.key(seed), 4)
    return {
        "probes": noise(seeds[0], (NV, NI, NX, NT), 1.0, 6.0, ((1, 32), (2, 16)), jnp.float32),
        "diffusion": draw_diffusion(jax.random.fold_in(seeds[3], 71), 0),
        "wavelet": noise(seeds[2], (TAPS,), TAPS ** -0.5, 1.0, (), jnp.float32),
    }


def wavelet_matrix(wavelet):
    offset = jnp.arange(NT)[None, :] - jnp.arange(NT)[:, None] + HALF
    onehot = (offset[:, :, None] == jnp.arange(2 * HALF + 1)[None, None, :]).astype(jnp.float32)
    return jnp.einsum("stk,k->st", onehot, wavelet.astype(jnp.float32), precision=lax.Precision.HIGHEST)


def data_term(volume, matrix):
    shape = volume.shape
    trace_rows = volume.reshape(-1, shape[-1])
    convolved = jnp.dot(trace_rows, matrix, precision=lax.Precision.HIGHEST)
    return jnp.dot(convolved, matrix.T, precision=lax.Precision.HIGHEST).reshape(shape)


def regularize(volume, tensor):
    padded = jnp.pad(volume, ((0, 1), (0, 1), (0, 0)))
    step_in = padded[1:, :-1] - volume
    step_x = padded[:-1, 1:] - volume
    flux_in = tensor[0] * step_in + tensor[1] * step_x
    flux_x = tensor[1] * step_in + tensor[2] * step_x
    lower_in = jnp.pad(flux_in, ((1, 0), (0, 0), (0, 0)))[:-1]
    lower_x = jnp.pad(flux_x, ((0, 0), (1, 0), (0, 0)))[:, :-1]
    return (lower_in - flux_in) + (lower_x - flux_x)


def reference(probes, diffusion, wavelet):
    matrix = wavelet_matrix(wavelet)
    tensor = diffusion.astype(jnp.float32)

    def damped(volume):
        return volume - 0.25 * (data_term(volume, matrix) + regularize(volume, tensor))

    def repeated(volume):
        for turn in range(2 * PAIRS):
            volume = damped(volume)
        return volume

    return lax.map(repeated, probes)
```

```python
import jax
import jax.numpy as jnp
from jax import lax
from jax.experimental import pallas as pl
from jax.experimental.pallas import tpu as pltpu
from jax.sharding import PartitionSpec as P

HALF = 20
STEPS = 6
NEAR = 2
F32, BF16 = jnp.float32, jnp.bfloat16
VMEM = pl.BlockSpec(memory_space=pltpu.VMEM)
HBM = pl.BlockSpec(memory_space=pl.ANY)


def pairing(value, axis, offset):
    count = lax.axis_size(axis)
    pairs = []
    for i in range(count):
        other = ((i + offset) ^ 1) - offset
        if 0 <= other < count:
            pairs.append((i, other))
    return lax.ppermute(value, axis, pairs)


def low_part(value):
    return value - value.astype(BF16).astype(F32)


def pieces_x(nv, nc):
    spans, start = {}, 0
    for v in range(nv):
        spans["u", v], start = start, start + STEPS
    for c in range(nc):
        spans["t", c], start = start, start + STEPS
    for v in range(nv):
        spans["low", v], start = start, start + NEAR
    return spans, start


def pieces_z(nv, nc, nx):
    wide = nx + 2 * STEPS
    spans, start = {}, 0
    for d in range(STEPS):
        for v in range(nv):
            spans["u", v, d], start = start, start + wide
        for c in range(nc):
            spans["t", c, d], start = start, start + wide
    for d in range(NEAR):
        for v in range(nv):
            spans["low", v, d], start = start, start + nx
    return spans, start


def padded(rows):
    return -(-rows // 16) * 16


def pack_x(probes, diffusion):
    nv, ni, nx, nt = probes.shape
    nc = diffusion.shape[0]
    spans, each = pieces_x(nv, nc)
    rows = ni * each
    tile = 8

    def kernel(u_hbm, t_hbm, even_ref, odd_ref, u, t, stage, sems):
        copies = []
        for k, first in enumerate((0, nx - tile)):
            copies.append(pltpu.make_async_copy(u_hbm.at[:, :, pl.ds(first, tile), :], u.at[k], sems.at[0, k]))
            copies.append(pltpu.make_async_copy(t_hbm.at[:, :, pl.ds(first, tile), :], t.at[k], sems.at[1, k]))
        for copy in copies:
            copy.start()
        for copy in copies:
            copy.wait()
        for side in range(2):
            first = 0 if side == 0 else tile - STEPS
            near = 0 if side == 0 else tile - NEAR
            for r in range(ni):
                base = r * each
                for v in range(nv):
                    start = base + spans["u", v]
                    stage[side, start : start + STEPS, :] = u[side, v, r, first : first + STEPS, :]
                    start = base + spans["low", v]
                    stage[side, start : start + NEAR, :] = low_part(u[side, v, r, near : near + NEAR, :])
                for c in range(nc):
                    start = base + spans["t", c]
                    stage[side, start : start + STEPS, :] = t[side, c, r, :, :].astype(F32)[first : first + STEPS]
        odd = lax.rem(lax.axis_index("xline"), 2)
        even_ref[...] = stage[1 - odd].astype(BF16)
        odd_ref[...] = stage[odd].astype(BF16)

    out = jax.ShapeDtypeStruct((rows, nt), BF16)
    return pl.pallas_call(
        kernel,
        out_shape=(out, out),
        in_specs=[HBM, HBM],
        out_specs=(VMEM, VMEM),
        scratch_shapes=[
            pltpu.VMEM((2, nv, ni, tile, nt), F32),
            pltpu.VMEM((2, nc, ni, tile, nt), BF16),
            pltpu.VMEM((2, rows, nt), F32),
            pltpu.SemaphoreType.DMA((2, 2)),
        ],
        compiler_params=pltpu.CompilerParams(vmem_limit_bytes=8 << 20),
        name="pack_x",
    )(probes, diffusion)


def gram(wavelet, nt):
    taps = wavelet.shape[0]

    def kernel(w_ref, g_ref, line):
        line[...] = jnp.zeros_like(line)
        line[0:1, 0:taps] = w_ref[...]
        source = lax.broadcasted_iota(jnp.int32, (nt, nt), 0)
        target = lax.broadcasted_iota(jnp.int32, (nt, nt), 1)
        middle = pltpu.roll(line[...], nt - HALF, 1)
        spread = jnp.broadcast_to(middle[0:1, :], (nt, nt))
        band = pltpu.roll(spread, 0, 1, stride=1, stride_axis=0)
        band = jnp.where(jnp.abs(target - source) <= HALF, band, 0.0)
        full = 0.25 * lax.dot_general(band, band, (((1,), (1,)), ((), ())), precision=lax.Precision.HIGHEST)
        high = full.astype(BF16)
        g_ref[0:nt, :] = high
        g_ref[nt : 2 * nt, :] = high
        g_ref[2 * nt : 3 * nt, :] = (full - high.astype(F32)).astype(BF16)

    return pl.pallas_call(
        kernel,
        out_shape=jax.ShapeDtypeStruct((3 * nt, nt), BF16),
        in_specs=[VMEM],
        out_specs=VMEM,
        scratch_shapes=[pltpu.VMEM((8, nt), F32)],
        compiler_params=pltpu.CompilerParams(vmem_limit_bytes=4 << 20),
        cost_estimate=pl.CostEstimate(flops=2 * nt**3, bytes_accessed=4 * nt * nt, transcendentals=0),
        name="gram",
    )(wavelet.reshape(1, taps))


def pack_z(probes, diffusion, even_x, odd_x):
    nv, ni, nx, nt = probes.shape
    nc = diffusion.shape[0]
    x_spans, x_each = pieces_x(nv, nc)
    spans, used = pieces_z(nv, nc, nx)
    rows = padded(used)

    def kernel(u, t, even_x_ref, odd_x_ref, even_ref, odd_ref, halo, stage):
        odd = lax.rem(lax.axis_index("xline"), 2)
        halo[1 - odd] = even_x_ref[...].astype(F32)
        halo[odd] = odd_x_ref[...].astype(F32)
        for side in range(2):
            if rows > used:
                stage[side, used:rows, :] = jnp.zeros((rows - used, nt), F32)
            for d in range(STEPS):
                r = d if side == 0 else ni - STEPS + d
                for kind, count, ref in (("u", nv, u), ("t", nc, t)):
                    for k in range(count):
                        start = spans[kind, k, d]
                        at = r * x_each + x_spans[kind, k]
                        stage[side, start : start + STEPS, :] = halo[0, at : at + STEPS, :]
                        stage[side, start + STEPS : start + STEPS + nx, :] = ref[k, r, :, :].astype(F32)
                        stage[side, start + STEPS + nx : start + 2 * STEPS + nx, :] = halo[1, at : at + STEPS, :]
            for d in range(NEAR):
                r = d if side == 0 else ni - NEAR + d
                for v in range(nv):
                    start = spans["low", v, d]
                    stage[side, start : start + nx, :] = low_part(u[v, r, :, :])
        odd = lax.rem(lax.axis_index("inline"), 2)
        even_ref[...] = stage[1 - odd].astype(BF16)
        odd_ref[...] = stage[odd].astype(BF16)

    out = jax.ShapeDtypeStruct((rows, nt), BF16)
    return pl.pallas_call(
        kernel,
        out_shape=(out, out),
        in_specs=[VMEM] * 4,
        out_specs=(VMEM, VMEM),
        scratch_shapes=[pltpu.VMEM((2, ni * x_each, nt), F32), pltpu.VMEM((2, rows, nt), F32)],
        compiler_params=pltpu.CompilerParams(vmem_limit_bytes=8 << 20),
        name="pack_z",
    )(probes, diffusion, even_x, odd_x)


def sweep(probes, diffusion, even_x, odd_x, even_z, odd_z, matrix):
    nv, ni, nx, nt = probes.shape
    nc = diffusion.shape[0]
    x_spans, x_each = pieces_x(nv, nc)
    z_spans, _ = pieces_z(nv, nc, nx)
    z_rows = even_z.shape[0]
    tile = 8
    height, width = ni + 2 * STEPS, nx + 2 * tile
    left, right = tile - STEPS, tile + nx
    chunk = 7

    def kernel(u0, t0, even_x_ref, odd_x_ref, even_z_ref, odd_z_ref, g_ref, out_hbm, u, t, halo_x, halo_z, data, sems):
        odd = lax.rem(lax.axis_index("xline"), 2)
        halo_x[1 - odd] = even_x_ref[...].astype(F32)
        halo_x[odd] = odd_x_ref[...].astype(F32)
        odd = lax.rem(lax.axis_index("inline"), 2)
        halo_z[1 - odd] = even_z_ref[...].astype(F32)
        halo_z[odd] = odd_z_ref[...].astype(F32)
        inside_in = lax.axis_index("inline") < lax.axis_size("inline") - 1
        inside_x = lax.axis_index("xline") < lax.axis_size("xline") - 1

        for v in range(nv):
            u[v, STEPS : STEPS + ni, tile : tile + nx, :] = u0[v]
        for c in range(nc):
            t[c, STEPS : STEPS + ni, tile : tile + nx, :] = 0.25 * t0[c].astype(F32)
        for r in range(ni):
            e, base = r + STEPS, r * x_each
            for side, first, near in ((0, left, STEPS - NEAR), (1, right, 0)):
                for v in range(nv):
                    at = base + x_spans["u", v]
                    u[v, e, first : first + STEPS, :] = halo_x[side, at : at + STEPS, :]
                    low = base + x_spans["low", v]
                    u[v, e, first + near : first + near + NEAR, :] = (
                        halo_x[side, at + near : at + near + NEAR, :] + halo_x[side, low : low + NEAR, :]
                    )
                for c in range(nc):
                    at = base + x_spans["t", c]
                    t[c, e, first : first + STEPS, :] = 0.25 * halo_x[side, at : at + STEPS, :]
        wide = nx + 2 * STEPS
        for side in range(2):
            for d in range(STEPS):
                e = d if side == 0 else STEPS + ni + d
                for v in range(nv):
                    at = z_spans["u", v, d]
                    u[v, e, left : left + wide, :] = halo_z[side, at : at + wide, :]
                for c in range(nc):
                    at = z_spans["t", c, d]
                    t[c, e, left : left + wide, :] = 0.25 * halo_z[side, at : at + wide, :]
            for d in range(NEAR):
                e = STEPS - NEAR + d if side == 0 else STEPS + ni + d
                for v in range(nv):
                    at = z_spans["low", v, d]
                    u[v, e, tile : tile + nx, :] = u[v, e, tile : tile + nx, :] + halo_z[side, at : at + nx, :]

        g = g_ref[...]
        tensor_of = lambda e: (t[0, e], t[1, e], t[2, e])
        copies = []
        for step in range(1, STEPS + 1):
            first, last = step, height - step
            before = []
            for v in range(nv):
                a, b, _ = tensor_of(first - 1)
                here = u[v, first - 1]
                step_x = pltpu.roll(here, width - 1, 0) - here
                before.append(a * (u[v, first] - here) + b * step_x)
            for low in range(first, last, chunk):
                high = min(low + chunk, last)
                count = high - low
                block = u[:, low:high].reshape(nv * count * width, nt)
                upper = block.astype(BF16)
                lower = (block - upper.astype(F32)).astype(BF16)
                parts = jnp.concatenate([upper, lower, upper], axis=1)
                data[0 : nv * count * width, :] = jnp.dot(parts, g, preferred_element_type=F32)
                for e in range(low, high):
                    a, b, c = tensor_of(e)
                    for v in range(nv):
                        here = u[v, e]
                        step_in = u[v, e + 1] - here
                        step_x = pltpu.roll(here, width - 1, 0) - here
                        flux_in = a * step_in + b * step_x
                        flux_x = b * step_in + c * step_x
                        start = (v * count + e - low) * width
                        turn = (flux_in - before[v]) + (flux_x - pltpu.roll(flux_x, 1, 0))
                        renewed = here - data[start : start + width, :] + turn
                        before[v] = flux_in
                        if e >= STEPS + ni:
                            renewed = jnp.where(inside_in, renewed, 0.0)
                        u[v, e, 0:right, :] = renewed[0:right]
                        u[v, e, right:width, :] = jnp.where(inside_x, renewed[right:width], 0.0)
                if step == STEPS:
                    r = low - STEPS
                    copy = pltpu.make_async_copy(
                        u.at[:, pl.ds(low, count), pl.ds(tile, nx), :],
                        out_hbm.at[:, pl.ds(r, count), :, :],
                        sems.at[len(copies)],
                    )
                    copy.start()
                    copies.append(copy)
        for copy in copies:
            copy.wait()

    return pl.pallas_call(
        kernel,
        out_shape=jax.ShapeDtypeStruct(probes.shape, F32),
        in_specs=[VMEM] * 7,
        out_specs=HBM,
        scratch_shapes=[
            pltpu.VMEM((nv, height, width, nt), F32),
            pltpu.VMEM((nc, height, width, nt), F32),
            pltpu.VMEM((2, ni * x_each, nt), F32),
            pltpu.VMEM((2, z_rows, nt), F32),
            pltpu.VMEM((nv * chunk * width, nt), F32),
            pltpu.SemaphoreType.DMA((8,)),
        ],
        compiler_params=pltpu.CompilerParams(vmem_limit_bytes=24 << 20),
        name="sweep",
    )(probes, diffusion, even_x, odd_x, even_z, odd_z, matrix)


def per_device(probes, diffusion, wavelet):
    even_x, odd_x = pack_x(probes, diffusion)
    even_x, odd_x = pairing(even_x, "xline", 0), pairing(odd_x, "xline", 1)
    matrix = gram(wavelet, probes.shape[-1])
    even_z, odd_z = pack_z(probes, diffusion, even_x, odd_x)
    even_z, odd_z = pairing(even_z, "inline", 0), pairing(odd_z, "inline", 1)
    return sweep(probes, diffusion, even_x, odd_x, even_z, odd_z, matrix)


def solution(mesh):
    return jax.shard_map(
        per_device,
        mesh=mesh,
        in_specs=(P(None, "inline", "xline", None), P(None, "inline", "xline", None), P()),
        out_specs=P(None, "inline", "xline", None),
        check_vma=False,
    )
```

```python
import jax
import jax.numpy as jnp
from jax import lax
from jax.experimental import pallas as pl
from jax.experimental.pallas import tpu as pltpu
from jax.sharding import PartitionSpec as P

HALF = 20
STEPS = 6
NEAR = 2
F32, BF16 = jnp.float32, jnp.bfloat16
VMEM = pl.BlockSpec(memory_space=pltpu.VMEM)
HBM = pl.BlockSpec(memory_space=pltpu.HBM)


def pairing(value, axis, offset):
    count = lax.axis_size(axis)
    pairs = []
    for i in range(count):
        other = ((i + offset) ^ 1) - offset
        if 0 <= other < count:
            pairs.append((i, other))
    return lax.ppermute(value, axis, pairs)


def low_part(value):
    return value - value.astype(BF16).astype(F32)


def pieces_x(nv, nc):
    spans, start = {}, 0
    for v in range(nv):
        spans["u", v], start = start, start + STEPS
    for c in range(nc):
        spans["t", c], start = start, start + STEPS
    for v in range(nv):
        spans["low", v], start = start, start + NEAR
    return spans, start


def pieces_z(nv, nc, nx):
    wide = nx + 2 * STEPS
    spans, start = {}, 0
    for d in range(STEPS):
        for v in range(nv):
            spans["u", v, d], start = start, start + wide
        for c in range(nc):
            spans["t", c, d], start = start, start + wide
    for d in range(NEAR):
        for v in range(nv):
            spans["low", v, d], start = start, start + nx
    return spans, start


def padded(rows):
    return -(-rows // 16) * 16


def parity(axis):
    return lax.rem(lax.axis_index(axis), 2)


def pieces_o(nv, nc):
    names = [("u", v, d) for d in range(STEPS) for v in range(nv)]
    names += [("low", v, d) for d in range(NEAR) for v in range(nv)]
    names += [("t", c, d) for c in range(nc) for d in range(STEPS)]
    return {name: k for k, name in enumerate(names)}


def pack_x(probes, diffusion):
    nv, ni, nx, nt = probes.shape
    nc = diffusion.shape[0]
    spans, each = pieces_x(nv, nc)
    o_pieces = pieces_o(nv, nc)
    rows, o_rows = ni * each, len(o_pieces) * nx
    tile = 8

    def kernel(u_hbm, t_hbm, even_ref, odd_ref, o_ref, u, t, u_o, stage, sems):
        odd_in = parity("inline")
        edge = odd_in * (ni - STEPS)
        copies = []
        for k, first in enumerate((0, nx - tile)):
            copies.append(pltpu.make_async_copy(u_hbm.at[:, :, pl.ds(first, tile), :], u.at[k], sems.at[0, k]))
            copies.append(pltpu.make_async_copy(t_hbm.at[:, :, pl.ds(first, tile), :], t.at[k], sems.at[1, k]))
        copies.append(pltpu.make_async_copy(u_hbm.at[:, pl.ds(edge, STEPS)], u_o, sems.at[2, 0]))
        for copy in copies:
            copy.start()
        direct = []
        for c in range(nc):
            at = o_pieces["t", c, 0] * nx
            for d in range(STEPS):
                copy = pltpu.make_async_copy(
                    t_hbm.at[c, edge + d], o_ref.at[pl.ds(at + d * nx, nx), :], sems.at[3 + c, d]
                )
                copy.start()
                direct.append(copy)
        for copy in copies:
            copy.wait()
        for side in range(2):
            first = 0 if side == 0 else tile - STEPS
            near = 0 if side == 0 else tile - NEAR
            for r in range(ni):
                base = r * each
                for v in range(nv):
                    start = base + spans["u", v]
                    stage[side, start : start + STEPS, :] = u[side, v, r, first : first + STEPS, :]
                    start = base + spans["low", v]
                    stage[side, start : start + NEAR, :] = low_part(u[side, v, r, near : near + NEAR, :])
                for c in range(nc):
                    start = base + spans["t", c]
                    stage[side, start : start + STEPS, :] = t[side, c, r, :, :].astype(F32)[first : first + STEPS]
        odd = parity("xline")
        even_ref[...] = stage[1 - odd].astype(BF16)
        odd_ref[...] = stage[odd].astype(BF16)
        near = odd_in * (STEPS - NEAR)
        for v in range(nv):
            for d in range(STEPS):
                at = o_pieces["u", v, d] * nx
                o_ref[at : at + nx, :] = u_o[v, d].astype(BF16)
            for d in range(NEAR):
                at = o_pieces["low", v, d] * nx
                o_ref[at : at + nx, :] = low_part(u_o[v, near + d]).astype(BF16)
        for copy in direct:
            copy.wait()

    out = jax.ShapeDtypeStruct((rows, nt), BF16)
    return pl.pallas_call(
        kernel,
        out_shape=(out, out, jax.ShapeDtypeStruct((o_rows, nt), BF16)),
        in_specs=[HBM, HBM],
        out_specs=(VMEM, VMEM, VMEM),
        scratch_shapes=[
            pltpu.VMEM((2, nv, ni, tile, nt), F32),
            pltpu.VMEM((2, nc, ni, tile, nt), BF16),
            pltpu.VMEM((nv, STEPS, nx, nt), F32),
            pltpu.VMEM((2, rows, nt), F32),
            pltpu.SemaphoreType.DMA((3 + nc, STEPS)),
        ],
        name="pack_x",
    )(probes, diffusion)


def gram(wavelet, nt):
    taps = wavelet.shape[0]

    def kernel(w_ref, g_ref, line):
        line[...] = jnp.zeros_like(line)
        line[0:1, 0:taps] = w_ref[...]
        source = lax.broadcasted_iota(jnp.int32, (nt, nt), 0)
        target = lax.broadcasted_iota(jnp.int32, (nt, nt), 1)
        middle = pltpu.roll(line[...], nt - HALF, 1)
        spread = jnp.broadcast_to(middle[0:1, :], (nt, nt))
        band = pltpu.roll(spread, 0, 1, stride=1, stride_axis=0)
        band = jnp.where(jnp.abs(target - source) <= HALF, band, 0.0)
        full = 0.25 * lax.dot_general(band, band, (((1,), (1,)), ((), ())), precision=lax.Precision.HIGHEST)
        high = full.astype(BF16)
        g_ref[0:nt, :] = high
        g_ref[nt : 2 * nt, :] = high
        g_ref[2 * nt : 3 * nt, :] = (full - high.astype(F32)).astype(BF16)

    return pl.pallas_call(
        kernel,
        out_shape=jax.ShapeDtypeStruct((3 * nt, nt), BF16),
        in_specs=[VMEM],
        out_specs=VMEM,
        scratch_shapes=[pltpu.VMEM((8, nt), F32)],
        compiler_params=pltpu.CompilerParams(vmem_limit_bytes=4 << 20),
        cost_estimate=pl.CostEstimate(flops=2 * nt**3, bytes_accessed=4 * nt * nt, transcendentals=0),
        name="gram",
    )(wavelet.reshape(1, taps))


def pack_z(probes, diffusion, even_x, odd_x):
    nv, ni, nx, nt = probes.shape
    nc = diffusion.shape[0]
    x_spans, x_each = pieces_x(nv, nc)
    spans, used = pieces_z(nv, nc, nx)
    corners, c_used = pieces_z(nv, nc, 0)
    rows, c_rows = padded(used), padded(c_used)

    def kernel(u, t, even_x_ref, odd_x_ref, e_ref, c_ref, halo, stage, stage_c):
        odd = parity("xline")
        halo[1 - odd] = even_x_ref[...].astype(F32)
        halo[odd] = odd_x_ref[...].astype(F32)
        for side in range(2):
            if rows > used:
                stage[side, used:rows, :] = jnp.zeros((rows - used, nt), F32)
            if c_rows > c_used:
                stage_c[side, c_used:c_rows, :] = jnp.zeros((c_rows - c_used, nt), F32)
            for d in range(STEPS):
                r = d if side == 0 else ni - STEPS + d
                for kind, count, ref in (("u", nv, u), ("t", nc, t)):
                    for k in range(count):
                        start = spans[kind, k, d]
                        at = r * x_each + x_spans[kind, k]
                        on_left, on_right = halo[0, at : at + STEPS, :], halo[1, at : at + STEPS, :]
                        stage[side, start : start + STEPS, :] = on_left
                        stage[side, start + STEPS : start + STEPS + nx, :] = ref[k, r, :, :].astype(F32)
                        stage[side, start + STEPS + nx : start + 2 * STEPS + nx, :] = on_right
                        start = corners[kind, k, d]
                        stage_c[side, start : start + STEPS, :] = on_left
                        stage_c[side, start + STEPS : start + 2 * STEPS, :] = on_right
            for d in range(NEAR):
                r = d if side == 0 else ni - NEAR + d
                for v in range(nv):
                    start = spans["low", v, d]
                    stage[side, start : start + nx, :] = low_part(u[v, r, :, :])
        odd = parity("inline")
        c_ref[...] = stage_c[odd].astype(BF16)
        e_ref[...] = stage[1 - odd].astype(BF16)

    return pl.pallas_call(
        kernel,
        out_shape=(jax.ShapeDtypeStruct((rows, nt), BF16), jax.ShapeDtypeStruct((c_rows, nt), BF16)),
        in_specs=[VMEM] * 4,
        out_specs=(VMEM, VMEM),
        scratch_shapes=[
            pltpu.VMEM((2, ni * x_each, nt), F32),
            pltpu.VMEM((2, rows, nt), F32),
            pltpu.VMEM((2, c_rows, nt), F32),
        ],
        compiler_params=pltpu.CompilerParams(vmem_limit_bytes=8 << 20),
        name="pack_z",
    )(probes, diffusion, even_x, odd_x)


def sweep(probes, diffusion, even_x, odd_x, e_rows, o_rows, c_rows, matrix):
    nv, ni, nx, nt = probes.shape
    nc = diffusion.shape[0]
    x_spans, x_each = pieces_x(nv, nc)
    z_spans, _ = pieces_z(nv, nc, nx)
    corners, _ = pieces_z(nv, nc, 0)
    o_pieces = pieces_o(nv, nc)
    tile = 8
    height, width = ni + 2 * STEPS, nx + 2 * tile
    left, right = tile - STEPS, tile + nx
    chunk = 7

    def kernel(u0, t0, even_x_ref, odd_x_ref, e_ref, o_ref, c_ref, g_ref, out_hbm, u, t, halo_x, halo_e, halo_c, data, sems):
        odd = parity("xline")
        halo_x[1 - odd] = even_x_ref[...].astype(F32)
        halo_x[odd] = odd_x_ref[...].astype(F32)
        halo_e[...] = e_ref[...].astype(F32)
        halo_c[...] = c_ref[...].astype(F32)
        odd_in = parity("inline")
        far = STEPS + ni
        e_first, o_first = (1 - odd_in) * far, odd_in * far
        e_near = e_first + odd_in * (STEPS - NEAR)
        o_near = o_first + (1 - odd_in) * (STEPS - NEAR)
        inside_in = lax.axis_index("inline") < lax.axis_size("inline") - 1
        inside_x = lax.axis_index("xline") < lax.axis_size("xline") - 1

        for v in range(nv):
            u[v, STEPS : STEPS + ni, tile : tile + nx, :] = u0[v]
        for c in range(nc):
            t[c, STEPS : STEPS + ni, tile : tile + nx, :] = 0.25 * t0[c].astype(F32)
        for r in range(ni):
            e, base = r + STEPS, r * x_each
            for side, first, near in ((0, left, STEPS - NEAR), (1, right, 0)):
                for v in range(nv):
                    at = base + x_spans["u", v]
                    u[v, e, first : first + STEPS, :] = halo_x[side, at : at + STEPS, :]
                    low = base + x_spans["low", v]
                    u[v, e, first + near : first + near + NEAR, :] = (
                        halo_x[side, at + near : at + near + NEAR, :] + halo_x[side, low : low + NEAR, :]
                    )
                for c in range(nc):
                    at = base + x_spans["t", c]
                    t[c, e, first : first + STEPS, :] = 0.25 * halo_x[side, at : at + STEPS, :]
        wide = nx + 2 * STEPS
        for d in range(STEPS):
            e, o = e_first + d, o_first + d
            for kind, count, ref, scale in (("u", nv, u, 1.0), ("t", nc, t, 0.25)):
                for k in range(count):
                    at = z_spans[kind, k, d]
                    ref[k, e, left : left + wide, :] = scale * halo_e[at : at + wide, :]
                    at = corners[kind, k, d]
                    ref[k, o, left : left + STEPS, :] = scale * halo_c[at : at + STEPS, :]
                    ref[k, o, right : right + STEPS, :] = scale * halo_c[at + STEPS : at + 2 * STEPS, :]
                    at = o_pieces[kind, k, d] * nx
                    ref[k, o, tile : tile + nx, :] = scale * o_ref[at : at + nx, :].astype(F32)
        for d in range(NEAR):
            e, o = e_near + d, o_near + d
            for v in range(nv):
                at = z_spans["low", v, d]
                u[v, e, tile : tile + nx, :] = u[v, e, tile : tile + nx, :] + halo_e[at : at + nx, :]
                at = o_pieces["low", v, d] * nx
                u[v, o, tile : tile + nx, :] = u[v, o, tile : tile + nx, :] + o_ref[at : at + nx, :].astype(F32)

        g = g_ref[...]
        tensor_of = lambda e: (t[0, e], t[1, e], t[2, e])
        copies = []
        for step in range(1, STEPS + 1):
            first, last = step, height - step
            before = []
            for v in range(nv):
                a, b, _ = tensor_of(first - 1)
                here = u[v, first - 1]
                step_x = pltpu.roll(here, width - 1, 0) - here
                before.append(a * (u[v, first] - here) + b * step_x)
            for low in range(first, last, chunk):
                high = min(low + chunk, last)
                count = high - low
                block = u[:, low:high].reshape(nv * count * width, nt)
                upper = block.astype(BF16)
                lower = (block - upper.astype(F32)).astype(BF16)
                parts = jnp.concatenate([upper, lower, upper], axis=1)
                data[0 : nv * count * width, :] = jnp.dot(parts, g, preferred_element_type=F32)
                for e in range(low, high):
                    a, b, c = tensor_of(e)
                    for v in range(nv):
                        here = u[v, e]
                        step_in = u[v, e + 1] - here
                        step_x = pltpu.roll(here, width - 1, 0) - here
                        flux_in = a * step_in + b * step_x
                        flux_x = b * step_in + c * step_x
                        start = (v * count + e - low) * width
                        turn = (flux_in - before[v]) + (flux_x - pltpu.roll(flux_x, 1, 0))
                        renewed = here - data[start : start + width, :] + turn
                        before[v] = flux_in
                        if e >= STEPS + ni:
                            renewed = jnp.where(inside_in, renewed, 0.0)
                        u[v, e, 0:right, :] = renewed[0:right]
                        u[v, e, right:width, :] = jnp.where(inside_x, renewed[right:width], 0.0)
                if step == STEPS:
                    r = low - STEPS
                    copy = pltpu.make_async_copy(
                        u.at[:, pl.ds(low, count), pl.ds(tile, nx), :],
                        out_hbm.at[:, pl.ds(r, count), :, :],
                        sems.at[len(copies)],
                    )
                    copy.start()
                    copies.append(copy)
        for copy in copies:
            copy.wait()

    return pl.pallas_call(
        kernel,
        out_shape=jax.ShapeDtypeStruct(probes.shape, F32),
        in_specs=[VMEM] * 8,
        out_specs=HBM,
        scratch_shapes=[
            pltpu.VMEM((nv, height, width, nt), F32),
            pltpu.VMEM((nc, height, width, nt), F32),
            pltpu.VMEM((2, ni * x_each, nt), F32),
            pltpu.VMEM((e_rows.shape[0], nt), F32),
            pltpu.VMEM((c_rows.shape[0], nt), F32),
            pltpu.VMEM((nv * chunk * width, nt), F32),
            pltpu.SemaphoreType.DMA((8,)),
        ],
        compiler_params=pltpu.CompilerParams(vmem_limit_bytes=24 << 20),
        name="sweep",
    )(probes, diffusion, even_x, odd_x, e_rows, o_rows, c_rows, matrix)


def per_device(probes, diffusion, wavelet):
    even_x, odd_x, o_rows = pack_x(probes, diffusion)
    odd_x = pairing(odd_x, "xline", 1)
    even_x = pairing(even_x, "xline", 0)
    o_rows = pairing(o_rows, "inline", 1)
    matrix = gram(wavelet, probes.shape[-1])
    e_rows, c_rows = pack_z(probes, diffusion, even_x, odd_x)
    c_rows = pairing(c_rows, "inline", 1)
    e_rows = pairing(e_rows, "inline", 0)
    return sweep(probes, diffusion, even_x, odd_x, e_rows, o_rows, c_rows, matrix)


def solution(mesh):
    return jax.shard_map(
        per_device,
        mesh=mesh,
        in_specs=(P(None, "inline", "xline", None), P(None, "inline", "xline", None), P()),
        out_specs=P(None, "inline", "xline", None),
        check_vma=False,
    )
```

```python
import jax
import jax.numpy as jnp
from jax import lax
from jax.experimental import pallas as pl
from jax.experimental.pallas import tpu as pltpu
from jax.sharding import PartitionSpec as P

HALF = 20
STEPS = 6
NEAR = 2
F32, BF16 = jnp.float32, jnp.bfloat16
VMEM = pl.BlockSpec(memory_space=pltpu.VMEM)
HBM = pl.BlockSpec(memory_space=pltpu.HBM)


def pairing(value, axis, offset):
    count = lax.axis_size(axis)
    pairs = []
    for i in range(count):
        other = ((i + offset) ^ 1) - offset
        if 0 <= other < count:
            pairs.append((i, other))
    return lax.ppermute(value, axis, pairs)


def low_part(value):
    return value - value.astype(BF16).astype(F32)


def pieces_x(nv, nc):
    spans, start = {}, 0
    for v in range(nv):
        spans["u", v], start = start, start + STEPS
    for c in range(nc):
        spans["t", c], start = start, start + STEPS
    for v in range(nv):
        spans["low", v], start = start, start + NEAR
    return spans, start


def pieces_z(nv, nc, nx):
    wide = nx + 2 * STEPS
    spans, start = {}, 0
    for d in range(STEPS):
        for v in range(nv):
            spans["u", v, d], start = start, start + wide
        for c in range(nc):
            spans["t", c, d], start = start, start + wide
    for d in range(NEAR):
        for v in range(nv):
            spans["low", v, d], start = start, start + nx
    return spans, start


def padded(rows):
    return -(-rows // 16) * 16


def parity(axis):
    return lax.rem(lax.axis_index(axis), 2)


def put_matrix(w, line, out):
    nt = line.shape[1]
    line[...] = jnp.zeros_like(line)
    line[0:1, 0 : w.shape[1]] = w[...]
    middle = pltpu.roll(line[...], nt - HALF, 1)
    source = lax.broadcasted_iota(jnp.int32, (nt, nt), 0)
    target = lax.broadcasted_iota(jnp.int32, (nt, nt), 1)
    band = pltpu.roll(jnp.broadcast_to(middle[0:1, :], (nt, nt)), 0, 1, stride=1, stride_axis=0)
    band = jnp.where(jnp.abs(target - source) <= HALF, band, 0.0)
    full = -0.25 * lax.dot_general(band, band, (((1,), (1,)), ((), ())), precision=lax.Precision.HIGHEST)
    full = jnp.where(source == target, 1.0 + full, full)
    high = full.astype(BF16)
    out[0:nt, 0:nt] = high
    out[nt : 2 * nt, 0:nt] = high
    out[0:nt, nt : 2 * nt] = (full - high.astype(F32)).astype(BF16)
    out[nt : 2 * nt, nt : 2 * nt] = jnp.zeros((nt, nt), BF16)


def pieces_o(nv, nc):
    names = [("u", v, d) for d in range(STEPS) for v in range(nv)]
    names += [("low", v, d) for d in range(NEAR) for v in range(nv)]
    names += [("t", c, d) for c in range(nc) for d in range(STEPS)]
    return {name: k for k, name in enumerate(names)}


def pack_x(probes, diffusion, wavelet):
    nv, ni, nx, nt = probes.shape
    nc = diffusion.shape[0]
    spans, each = pieces_x(nv, nc)
    o_pieces = pieces_o(nv, nc)
    rows = ni * each

    def kernel(u_hbm, t_hbm, w_hbm, even_ref, odd_ref, o_ref, u, t, g, stage, w, line, sems):
        taps = pltpu.make_async_copy(w_hbm, w, sems.at[nv + nc])
        taps.start()
        copies = []
        for source, target in ((u_hbm, u), (t_hbm, t)):
            for k in range(source.shape[0]):
                copies.append(pltpu.make_async_copy(source.at[k], target.at[k], sems.at[len(copies)]))
        for copy in copies:
            copy.start()
        taps.wait()
        put_matrix(w, line, g)
        for copy in copies:
            copy.wait()
        for side in range(2):
            first = 0 if side == 0 else nx - STEPS
            near = 0 if side == 0 else nx - NEAR
            tile = 0 if side == 0 else nx - 8
            for r in range(ni):
                base = r * each
                for v in range(nv):
                    start = base + spans["u", v]
                    stage[side, start : start + STEPS, :] = u[v, r, first : first + STEPS, :]
                    start = base + spans["low", v]
                    stage[side, start : start + NEAR, :] = low_part(u[v, r, near : near + NEAR, :])
                for c in range(nc):
                    start = base + spans["t", c]
                    edge = t[c, r, tile : tile + 8, :].astype(F32)
                    stage[side, start : start + STEPS, :] = edge[first - tile : first - tile + STEPS]
        odd = parity("xline")
        even_ref[...] = stage[1 - odd].astype(BF16)
        odd_ref[...] = stage[odd].astype(BF16)

        odd = parity("inline")
        edge, near = odd * (ni - STEPS), odd * (STEPS - NEAR)
        for d in range(STEPS):
            for v in range(nv):
                at = o_pieces["u", v, d] * nx
                o_ref[at : at + nx, :] = u[v, edge + d].astype(BF16)
            for c in range(nc):
                at = o_pieces["t", c, d] * nx
                o_ref[at : at + nx, :] = t[c, edge + d]
        for d in range(NEAR):
            for v in range(nv):
                at = o_pieces["low", v, d] * nx
                o_ref[at : at + nx, :] = low_part(u[v, edge + near + d]).astype(BF16)

    out = jax.ShapeDtypeStruct((rows, nt), BF16)
    return pl.pallas_call(
        kernel,
        out_shape=(
            out,
            out,
            jax.ShapeDtypeStruct((len(o_pieces) * nx, nt), BF16),
            jax.ShapeDtypeStruct(probes.shape, F32),
            jax.ShapeDtypeStruct(diffusion.shape, BF16),
            jax.ShapeDtypeStruct((2 * nt, 2 * nt), BF16),
        ),
        in_specs=[HBM] * 3,
        out_specs=(VMEM,) * 6,
        scratch_shapes=[
            pltpu.VMEM((2, rows, nt), F32),
            pltpu.VMEM((1, wavelet.shape[0]), F32),
            pltpu.VMEM((8, nt), F32),
            pltpu.SemaphoreType.DMA((nv + nc + 1,)),
        ],
        compiler_params=pltpu.CompilerParams(vmem_limit_bytes=4 << 20),
        name="pack_x",
    )(*(pltpu.with_memory_space_constraint(x, pltpu.HBM) for x in (probes, diffusion, wavelet.reshape(1, -1))))


def pack_z(probes, diffusion, even_x, odd_x):
    nv, ni, nx, nt = probes.shape
    nc = diffusion.shape[0]
    x_spans, x_each = pieces_x(nv, nc)
    spans, used = pieces_z(nv, nc, nx)
    corners, c_used = pieces_z(nv, nc, 0)
    rows, c_rows = padded(used), padded(c_used)

    def kernel(u, t, even_x_ref, odd_x_ref, e_ref, c_ref, halo, stage, stage_c):
        odd = parity("xline")
        halo[1 - odd] = even_x_ref[...].astype(F32)
        halo[odd] = odd_x_ref[...].astype(F32)
        for side in range(2):
            if rows > used:
                stage[side, used:rows, :] = jnp.zeros((rows - used, nt), F32)
            if c_rows > c_used:
                stage_c[side, c_used:c_rows, :] = jnp.zeros((c_rows - c_used, nt), F32)
            for d in range(STEPS):
                r = d if side == 0 else ni - STEPS + d
                for kind, count, ref in (("u", nv, u), ("t", nc, t)):
                    for k in range(count):
                        start = spans[kind, k, d]
                        at = r * x_each + x_spans[kind, k]
                        on_left, on_right = halo[0, at : at + STEPS, :], halo[1, at : at + STEPS, :]
                        stage[side, start : start + STEPS, :] = on_left
                        stage[side, start + STEPS : start + STEPS + nx, :] = ref[k, r, :, :].astype(F32)
                        stage[side, start + STEPS + nx : start + 2 * STEPS + nx, :] = on_right
                        start = corners[kind, k, d]
                        stage_c[side, start : start + STEPS, :] = on_left
                        stage_c[side, start + STEPS : start + 2 * STEPS, :] = on_right
            for d in range(NEAR):
                r = d if side == 0 else ni - NEAR + d
                for v in range(nv):
                    start = spans["low", v, d]
                    stage[side, start : start + nx, :] = low_part(u[v, r, :, :])
        odd = parity("inline")
        c_ref[...] = stage_c[odd].astype(BF16)
        e_ref[...] = stage[1 - odd].astype(BF16)

    return pl.pallas_call(
        kernel,
        out_shape=(jax.ShapeDtypeStruct((rows, nt), BF16), jax.ShapeDtypeStruct((c_rows, nt), BF16)),
        in_specs=[VMEM] * 4,
        out_specs=(VMEM, VMEM),
        scratch_shapes=[
            pltpu.VMEM((2, ni * x_each, nt), F32),
            pltpu.VMEM((2, rows, nt), F32),
            pltpu.VMEM((2, c_rows, nt), F32),
        ],
        compiler_params=pltpu.CompilerParams(vmem_limit_bytes=8 << 20),
        name="pack_z",
    )(probes, diffusion, even_x, odd_x)


EDGE = 8


def lay_out(probes, diffusion, even_x, odd_x):
    nv, ni, nx, nt = probes.shape
    nc = diffusion.shape[0]
    spans, each = pieces_x(nv, nc)
    height, width = ni + 2 * STEPS, nx + 3 * EDGE

    def kernel(u0, t0, even_ref, odd_ref, u, t, halo):
        odd = parity("xline")
        halo[1 - odd] = even_ref[...].astype(F32)
        halo[odd] = odd_ref[...].astype(F32)
        for v in range(nv):
            u[v, STEPS : STEPS + ni, EDGE : EDGE + nx, :] = u0[v]
        for c in range(nc):
            t[c, STEPS : STEPS + ni, EDGE : EDGE + nx, :] = 0.25 * t0[c].astype(F32)
        for r in range(ni):
            e, base = r + STEPS, r * each
            for side, first, near in ((0, EDGE - STEPS, STEPS - NEAR), (1, EDGE + nx, 0)):
                for v in range(nv):
                    at, low = base + spans["u", v], base + spans["low", v]
                    u[v, e, first : first + STEPS, :] = halo[side, at : at + STEPS, :]
                    u[v, e, first + near : first + near + NEAR, :] = (
                        halo[side, at + near : at + near + NEAR, :] + halo[side, low : low + NEAR, :]
                    )
                for c in range(nc):
                    at = base + spans["t", c]
                    t[c, e, first : first + STEPS, :] = 0.25 * halo[side, at : at + STEPS, :]

    return pl.pallas_call(
        kernel,
        out_shape=(
            jax.ShapeDtypeStruct((nv, height + STEPS, width, nt), F32),
            jax.ShapeDtypeStruct((nc, height, width, nt), F32),
        ),
        in_specs=[VMEM] * 4,
        out_specs=(VMEM, VMEM),
        scratch_shapes=[pltpu.VMEM((2, ni * each, nt), F32)],
        compiler_params=pltpu.CompilerParams(vmem_limit_bytes=4 << 20),
        cost_estimate=pl.CostEstimate(flops=1 << 20, bytes_accessed=4 << 20, transcendentals=0),
        name="lay_out",
    )(probes, diffusion, even_x, odd_x)


def take_rows(first, high_side, message, halo, u, t, nx):
    spans, _ = pieces_z(u.shape[0], t.shape[0], nx)
    halo[...] = message[...].astype(F32)
    left, wide = EDGE - STEPS, nx + 2 * STEPS
    near = 0 if high_side else STEPS - NEAR
    for d in range(STEPS):
        for v in range(u.shape[0]):
            at = spans["u", v, d]
            u[v, first + d, left : left + wide, :] = halo[at : at + wide, :]
        for c in range(t.shape[0]):
            at = spans["t", c, d]
            t[c, first + d, left : left + wide, :] = 0.25 * halo[at : at + wide, :]
    for d in range(NEAR):
        for v in range(u.shape[0]):
            at, e = spans["low", v, d], first + near + d
            u[v, e, EDGE : EDGE + nx, :] = u[v, e, EDGE : EDGE + nx, :] + halo[at : at + nx, :]


def take_split_rows(first, high_side, rows, corners, halo, u, t, nx):
    spans, _ = pieces_z(u.shape[0], t.shape[0], 0)
    pieces = pieces_o(u.shape[0], t.shape[0])
    halo[...] = corners[...].astype(F32)
    near = 0 if high_side else STEPS - NEAR
    for d in range(STEPS):
        for kind, ref, scale in (("u", u, 1.0), ("t", t, 0.25)):
            for k in range(ref.shape[0]):
                at = spans[kind, k, d]
                ref[k, first + d, EDGE - STEPS : EDGE, :] = scale * halo[at : at + STEPS, :]
                ref[k, first + d, EDGE + nx : EDGE + nx + STEPS, :] = scale * halo[at + STEPS : at + 2 * STEPS, :]
                at = pieces[kind, k, d] * nx
                whole = rows[at : at + nx, :].astype(F32)
                if kind == "u" and near <= d < near + NEAR:
                    at = pieces["low", k, d - near] * nx
                    whole = whole + rows[at : at + nx, :].astype(F32)
                ref[k, first + d, EDGE : EDGE + nx, :] = scale * whole


def advance(step, first, count, above, below, refs, inside_x, inside_in, beyond, nx):
    u, t, g, data, cross = refs
    nv, nt = u.shape[0], u.shape[3]
    start, wide = (2, nx + 16) if step <= 2 else (4, nx + 8)
    window = slice(start, start + wide)
    tiles = [slice(at, at + TILE) for at in range(start, start + wide, TILE)]
    right_of = lambda cols: slice(cols.start + 1, cols.stop + 1)
    keeps = {}
    for cols in tiles:
        if cols.stop > EDGE + nx:
            column = lax.broadcasted_iota(jnp.int32, (TILE, nt), 0) + cols.start
            keeps[cols.start] = jnp.logical_or(column < EDGE + nx, inside_x)
    before = {}
    last = first + count
    for low in range(first, last, CHUNK):
        high = min(low + CHUNK, last)
        rows = nv * (high - low) * wide
        block = u[:, low:high, window, :].reshape(rows, nt)
        upper = block.astype(BF16)
        lower = (block - upper.astype(F32)).astype(BF16)
        both = jnp.dot(jnp.concatenate([upper, lower], axis=1), g, preferred_element_type=F32)
        data[0:rows, :] = both[:, 0:nt] + both[:, nt : 2 * nt]
        for cols in tiles:
            right = right_of(cols)
            for v in range(nv):
                if low == first:
                    here = u[v, above, cols, :]
                    a, b = t[0, first - 1, cols, :], t[1, first - 1, cols, :]
                    before[v, cols.start] = a * (u[v, first, cols, :] - here) + b * (u[v, above, right, :] - here)
            for e in range(low, high):
                after = below if e == last - 1 else e + 1
                a, b, c = t[0, e, cols, :], t[1, e, cols, :], t[2, e, cols, :]
                for v in range(nv):
                    here = u[v, e, cols, :]
                    step_in = u[v, after, cols, :] - here
                    step_x = u[v, e, right, :] - here
                    flux_in = a * step_in + b * step_x
                    flux_x = b * step_in + c * step_x
                    slot, at = (e - low) * nv + v, 8 + cols.start - start
                    cross[slot, at : at + TILE, :] = flux_x
                    turn = (flux_in - before[v, cols.start]) + (flux_x - cross[slot, at - 1 : at - 1 + TILE, :])
                    at = (v * (high - low) + e - low) * wide + cols.start - start
                    renewed = data[at : at + TILE, :] + turn
                    before[v, cols.start] = flux_in
                    if e >= beyond:
                        renewed = jnp.where(inside_in, renewed, 0.0)
                    if cols.start in keeps:
                        renewed = jnp.where(keeps[cols.start], renewed, 0.0)
                    u[v, e, cols, :] = renewed


TILE = 8
CHUNK = 20


def sweep_scratch(message_rows, nv, nx, nt):
    return [
        pltpu.VMEM((message_rows, nt), F32),
        pltpu.VMEM((nv * CHUNK * (nx + 16), nt), F32),
        pltpu.VMEM((CHUNK * nv, nx + 24, nt), F32),
    ]


def inner(axis):
    return lax.axis_index(axis) < lax.axis_size(axis) - 1


def sweep_far(u, t, message, matrix, ni, nx):
    nv, _, _, nt = u.shape
    height = ni + 2 * STEPS

    def kernel(u_in, t_in, message_ref, g_ref, u, t, halo, data, cross):
        inside_x = inner("xline")
        refs = (u, t, g_ref[...], data, cross)

        def run(odd):
            take_rows(0 if odd else STEPS + ni, not odd, message_ref, halo, u, t, nx)
            for step in range(1, STEPS + 1):
                first = step if odd else STEPS + step
                count = ni + STEPS - 2 * step
                border = first + count - 1 if odd else first
                for v in range(nv):
                    u[v, height + step - 1] = u[v, border]
                advance(step, first, count, first - 1, first + count, refs, inside_x, None, height, nx)

        odd = parity("inline")
        pl.when(odd == 0)(lambda: run(False))
        pl.when(odd == 1)(lambda: run(True))

    return pl.pallas_call(
        kernel,
        out_shape=(jax.ShapeDtypeStruct(u.shape, F32), jax.ShapeDtypeStruct(t.shape, F32)),
        in_specs=[VMEM] * 4,
        out_specs=(VMEM, VMEM),
        input_output_aliases={0: 0, 1: 1},
        scratch_shapes=sweep_scratch(message.shape[0], nv, nx, nt),
        compiler_params=pltpu.CompilerParams(vmem_limit_bytes=8 << 20),
        cost_estimate=pl.CostEstimate(flops=1 << 28, bytes_accessed=16 << 20, transcendentals=0),
        name="sweep_far",
    )(u, t, message, matrix)


def sweep_near(u, t, message, corners, matrix, ni, nx):
    nv, _, _, nt = u.shape
    height = ni + 2 * STEPS

    def kernel(u_in, t_in, message_ref, corners_ref, g_ref, out_hbm, u, t, halo, data, cross, sems):
        inside_x, inside_in = inner("xline"), inner("inline")
        refs = (u, t, g_ref[...], data, cross)

        def result(row, count, k):
            source = u.at[:, pl.ds(STEPS + row, count), pl.ds(EDGE, nx), :]
            return pltpu.make_async_copy(source, out_hbm.at[:, pl.ds(row, count), :, :], sems.at[k])

        def run(odd):
            ready = result(0 if odd else STEPS, ni - STEPS, 0)
            ready.start()
            take_split_rows(STEPS + ni if odd else 0, odd, message_ref, corners_ref, halo, u, t, nx)
            for step in range(1, STEPS + 1):
                first = STEPS + ni - step if odd else step
                kept = height + step - 1
                above = kept if odd else first - 1
                below = first + STEPS if odd else kept
                advance(step, first, STEPS, above, below, refs, inside_x, inside_in, STEPS + ni if odd else height, nx)
            rest = result(ni - STEPS if odd else 0, STEPS, 1)
            rest.start()
            ready.wait()
            rest.wait()

        odd = parity("inline")
        pl.when(odd == 0)(lambda: run(False))
        pl.when(odd == 1)(lambda: run(True))

    out = pl.pallas_call(
        kernel,
        out_shape=(
            jax.ShapeDtypeStruct((nv, ni, nx, nt), F32),
            jax.ShapeDtypeStruct(u.shape, F32),
            jax.ShapeDtypeStruct(t.shape, F32),
        ),
        in_specs=[VMEM] * 5,
        out_specs=(HBM, VMEM, VMEM),
        input_output_aliases={0: 1, 1: 2},
        scratch_shapes=sweep_scratch(corners.shape[0], nv, nx, nt) + [pltpu.SemaphoreType.DMA((2,))],
        compiler_params=pltpu.CompilerParams(vmem_limit_bytes=8 << 20),
        name="sweep_near",
    )(u, t, message, corners, matrix)
    return out[0]


def per_device(probes, diffusion, wavelet):
    _, ni, nx, _ = probes.shape
    even_x, odd_x, o_rows, probes, diffusion, matrix = pack_x(probes, diffusion, wavelet)
    odd_x = pairing(odd_x, "xline", 1)
    even_x = pairing(even_x, "xline", 0)
    o_rows = pairing(o_rows, "inline", 1)
    e_rows, corners = pack_z(probes, diffusion, even_x, odd_x)
    e_rows = pairing(e_rows, "inline", 0)
    corners = pairing(corners, "inline", 1)
    u, t = lay_out(probes, diffusion, even_x, odd_x)
    u, t = sweep_far(u, t, e_rows, matrix, ni, nx)
    return sweep_near(u, t, o_rows, corners, matrix, ni, nx)


def solution(mesh):
    return jax.shard_map(
        per_device,
        mesh=mesh,
        in_specs=(P(None, "inline", "xline", None), P(None, "inline", "xline", None), P()),
        out_specs=P(None, "inline", "xline", None),
        check_vma=False,
    )
```

```python
import jax
import jax.numpy as jnp
from jax import lax
from jax.experimental import pallas as pl
from jax.experimental.pallas import tpu as pltpu
from jax.sharding import PartitionSpec as P

HALF = 20
STEPS = 6
NEAR = 2
F32, BF16 = jnp.float32, jnp.bfloat16
VMEM = pl.BlockSpec(memory_space=pltpu.VMEM)
HBM = pl.BlockSpec(memory_space=pltpu.HBM)


def pairing(value, axis, offset):
    count = lax.axis_size(axis)
    pairs = []
    for i in range(count):
        other = ((i + offset) ^ 1) - offset
        if 0 <= other < count:
            pairs.append((i, other))
    return lax.ppermute(value, axis, pairs)


def low_part(value):
    return value - value.astype(BF16).astype(F32)


def pieces_x(nv, nc):
    spans, start = {}, 0
    for v in range(nv):
        spans["u", v], start = start, start + STEPS
    for c in range(nc):
        spans["t", c], start = start, start + STEPS
    for v in range(nv):
        spans["low", v], start = start, start + NEAR
    return spans, start


def pieces_z(nv, nc, nx):
    wide = nx + 2 * STEPS
    spans, start = {}, 0
    for d in range(STEPS):
        for v in range(nv):
            spans["u", v, d], start = start, start + wide
        for c in range(nc):
            spans["t", c, d], start = start, start + wide
    for d in range(NEAR):
        for v in range(nv):
            spans["low", v, d], start = start, start + nx
    return spans, start


def padded(rows):
    return -(-rows // 16) * 16


def parity(axis):
    return lax.rem(lax.axis_index(axis), 2)


def put_matrix(w, line, out):
    nt = line.shape[1]
    line[...] = jnp.zeros_like(line)
    line[0:1, 0 : w.shape[1]] = w[...]
    middle = pltpu.roll(line[...], nt - HALF, 1)
    source = lax.broadcasted_iota(jnp.int32, (nt, nt), 0)
    target = lax.broadcasted_iota(jnp.int32, (nt, nt), 1)
    band = pltpu.roll(jnp.broadcast_to(middle[0:1, :], (nt, nt)), 0, 1, stride=1, stride_axis=0)
    band = jnp.where(jnp.abs(target - source) <= HALF, band, 0.0)
    full = -0.25 * lax.dot_general(band, band, (((1,), (1,)), ((), ())), precision=lax.Precision.HIGHEST)
    full = jnp.where(source == target, 1.0 + full, full)
    high = full.astype(BF16)
    out[0:nt, 0:nt] = high
    out[nt : 2 * nt, 0:nt] = high
    out[0:nt, nt : 2 * nt] = (full - high.astype(F32)).astype(BF16)
    out[nt : 2 * nt, nt : 2 * nt] = jnp.zeros((nt, nt), BF16)


def pieces_o(nv, nc):
    names = [("u", v, d) for d in range(STEPS) for v in range(nv)]
    names += [("low", v, d) for d in range(NEAR) for v in range(nv)]
    names += [("t", c, d) for c in range(nc) for d in range(STEPS)]
    return {name: k for k, name in enumerate(names)}


def pack_x(probes, diffusion, wavelet):
    nv, ni, nx, nt = probes.shape
    nc = diffusion.shape[0]
    spans, each = pieces_x(nv, nc)
    o_pieces = pieces_o(nv, nc)
    rows = ni * each

    def kernel(u_hbm, t_hbm, w_hbm, even_ref, odd_ref, o_ref, u, t, g, stage, w, line, sems):
        taps = pltpu.make_async_copy(w_hbm, w, sems.at[6])
        taps.start()
        edges, middle = [], []
        for spans_of, copies in ((((0, 8), (nx - 8, 8)), edges), (((8, nx - 16),), middle)):
            for first, count in spans_of:
                for source, target in ((u_hbm, u), (t_hbm, t)):
                    part = (slice(None), slice(None), pl.ds(first, count), slice(None))
                    sem = sems.at[len(edges) + len(middle)]
                    copies.append(pltpu.make_async_copy(source.at[part], target.at[part], sem))
        for copy in edges + middle:
            copy.start()
        taps.wait()
        put_matrix(w, line, g)
        for copy in edges:
            copy.wait()
        for side in range(2):
            first = 0 if side == 0 else nx - STEPS
            near = 0 if side == 0 else nx - NEAR
            tile = 0 if side == 0 else nx - 8
            for r in range(ni):
                base = r * each
                for v in range(nv):
                    start = base + spans["u", v]
                    stage[side, start : start + STEPS, :] = u[v, r, first : first + STEPS, :]
                    start = base + spans["low", v]
                    stage[side, start : start + NEAR, :] = low_part(u[v, r, near : near + NEAR, :])
                for c in range(nc):
                    start = base + spans["t", c]
                    edge = t[c, r, tile : tile + 8, :].astype(F32)
                    stage[side, start : start + STEPS, :] = edge[first - tile : first - tile + STEPS]
        odd = parity("xline")
        even_ref[...] = stage[1 - odd].astype(BF16)
        odd_ref[...] = stage[odd].astype(BF16)

        for copy in middle:
            copy.wait()
        odd = parity("inline")
        edge, near = odd * (ni - STEPS), odd * (STEPS - NEAR)
        for d in range(STEPS):
            for v in range(nv):
                at = o_pieces["u", v, d] * nx
                o_ref[at : at + nx, :] = u[v, edge + d].astype(BF16)
            for c in range(nc):
                at = o_pieces["t", c, d] * nx
                o_ref[at : at + nx, :] = t[c, edge + d]
        for d in range(NEAR):
            for v in range(nv):
                at = o_pieces["low", v, d] * nx
                o_ref[at : at + nx, :] = low_part(u[v, edge + near + d]).astype(BF16)

    out = jax.ShapeDtypeStruct((rows, nt), BF16)
    return pl.pallas_call(
        kernel,
        out_shape=(
            out,
            out,
            jax.ShapeDtypeStruct((len(o_pieces) * nx, nt), BF16),
            jax.ShapeDtypeStruct(probes.shape, F32),
            jax.ShapeDtypeStruct(diffusion.shape, BF16),
            jax.ShapeDtypeStruct((2 * nt, 2 * nt), BF16),
        ),
        in_specs=[HBM] * 3,
        out_specs=(VMEM,) * 6,
        scratch_shapes=[
            pltpu.VMEM((2, rows, nt), F32),
            pltpu.VMEM((1, wavelet.shape[0]), F32),
            pltpu.VMEM((8, nt), F32),
            pltpu.SemaphoreType.DMA((7,)),
        ],
        compiler_params=pltpu.CompilerParams(vmem_limit_bytes=4 << 20),
        name="pack_x",
    )(*(pltpu.with_memory_space_constraint(x, pltpu.HBM) for x in (probes, diffusion, wavelet.reshape(1, -1))))


def pack_z(probes, diffusion, even_x, odd_x):
    nv, ni, nx, nt = probes.shape
    nc = diffusion.shape[0]
    x_spans, x_each = pieces_x(nv, nc)
    spans, used = pieces_z(nv, nc, nx)
    corners, c_used = pieces_z(nv, nc, 0)
    rows, c_rows = padded(used), padded(c_used)

    def kernel(u, t, even_x_ref, odd_x_ref, e_ref, c_ref, halo, stage, stage_c):
        odd = parity("xline")
        halo[1 - odd] = even_x_ref[...].astype(F32)
        halo[odd] = odd_x_ref[...].astype(F32)
        for side in range(2):
            if rows > used:
                stage[side, used:rows, :] = jnp.zeros((rows - used, nt), F32)
            if c_rows > c_used:
                stage_c[side, c_used:c_rows, :] = jnp.zeros((c_rows - c_used, nt), F32)
            for d in range(STEPS):
                r = d if side == 0 else ni - STEPS + d
                for kind, count, ref in (("u", nv, u), ("t", nc, t)):
                    for k in range(count):
                        start = spans[kind, k, d]
                        at = r * x_each + x_spans[kind, k]
                        on_left, on_right = halo[0, at : at + STEPS, :], halo[1, at : at + STEPS, :]
                        stage[side, start : start + STEPS, :] = on_left
                        stage[side, start + STEPS : start + STEPS + nx, :] = ref[k, r, :, :].astype(F32)
                        stage[side, start + STEPS + nx : start + 2 * STEPS + nx, :] = on_right
                        start = corners[kind, k, d]
                        stage_c[side, start : start + STEPS, :] = on_left
                        stage_c[side, start + STEPS : start + 2 * STEPS, :] = on_right
            for d in range(NEAR):
                r = d if side == 0 else ni - NEAR + d
                for v in range(nv):
                    start = spans["low", v, d]
                    stage[side, start : start + nx, :] = low_part(u[v, r, :, :])
        odd = parity("inline")
        c_ref[...] = stage_c[odd].astype(BF16)
        e_ref[...] = stage[1 - odd].astype(BF16)

    return pl.pallas_call(
        kernel,
        out_shape=(jax.ShapeDtypeStruct((rows, nt), BF16), jax.ShapeDtypeStruct((c_rows, nt), BF16)),
        in_specs=[VMEM] * 4,
        out_specs=(VMEM, VMEM),
        scratch_shapes=[
            pltpu.VMEM((2, ni * x_each, nt), F32),
            pltpu.VMEM((2, rows, nt), F32),
            pltpu.VMEM((2, c_rows, nt), F32),
        ],
        compiler_params=pltpu.CompilerParams(vmem_limit_bytes=8 << 20),
        name="pack_z",
    )(probes, diffusion, even_x, odd_x)


EDGE = 8


def lay_out(u0, t0, even_ref, odd_ref, u, t, halo):
    nv, ni, nx, _ = u0.shape
    nc = t0.shape[0]
    spans, each = pieces_x(nv, nc)
    odd = parity("xline")
    halo[1 - odd] = even_ref[...].astype(F32)
    halo[odd] = odd_ref[...].astype(F32)
    for v in range(nv):
        u[v, STEPS : STEPS + ni, EDGE : EDGE + nx, :] = u0[v]
    for c in range(nc):
        t[c, STEPS : STEPS + ni, EDGE : EDGE + nx, :] = 0.25 * t0[c].astype(F32)
    for r in range(ni):
        e, base = r + STEPS, r * each
        for side, first, near in ((0, EDGE - STEPS, STEPS - NEAR), (1, EDGE + nx, 0)):
            for v in range(nv):
                at, low = base + spans["u", v], base + spans["low", v]
                u[v, e, first : first + STEPS, :] = halo[side, at : at + STEPS, :]
                u[v, e, first + near : first + near + NEAR, :] = (
                    halo[side, at + near : at + near + NEAR, :] + halo[side, low : low + NEAR, :]
                )
            for c in range(nc):
                at = base + spans["t", c]
                t[c, e, first : first + STEPS, :] = 0.25 * halo[side, at : at + STEPS, :]


def take_rows(first, high_side, message, halo, u, t, nx):
    spans, _ = pieces_z(u.shape[0], t.shape[0], nx)
    halo[...] = message[...].astype(F32)
    left, wide = EDGE - STEPS, nx + 2 * STEPS
    near = 0 if high_side else STEPS - NEAR
    for d in range(STEPS):
        for v in range(u.shape[0]):
            at = spans["u", v, d]
            u[v, first + d, left : left + wide, :] = halo[at : at + wide, :]
        for c in range(t.shape[0]):
            at = spans["t", c, d]
            t[c, first + d, left : left + wide, :] = 0.25 * halo[at : at + wide, :]
    for d in range(NEAR):
        for v in range(u.shape[0]):
            at, e = spans["low", v, d], first + near + d
            u[v, e, EDGE : EDGE + nx, :] = u[v, e, EDGE : EDGE + nx, :] + halo[at : at + nx, :]


def take_split_rows(first, high_side, rows, corners, halo, u, t, nx):
    spans, _ = pieces_z(u.shape[0], t.shape[0], 0)
    pieces = pieces_o(u.shape[0], t.shape[0])
    halo[...] = corners[...].astype(F32)
    near = 0 if high_side else STEPS - NEAR
    for d in range(STEPS):
        for kind, ref, scale in (("u", u, 1.0), ("t", t, 0.25)):
            for k in range(ref.shape[0]):
                at = spans[kind, k, d]
                ref[k, first + d, EDGE - STEPS : EDGE, :] = scale * halo[at : at + STEPS, :]
                ref[k, first + d, EDGE + nx : EDGE + nx + STEPS, :] = scale * halo[at + STEPS : at + 2 * STEPS, :]
                at = pieces[kind, k, d] * nx
                whole = rows[at : at + nx, :].astype(F32)
                if kind == "u" and near <= d < near + NEAR:
                    at = pieces["low", k, d - near] * nx
                    whole = whole + rows[at : at + nx, :].astype(F32)
                ref[k, first + d, EDGE : EDGE + nx, :] = scale * whole


def advance(step, first, count, above, below, refs, inside_x, inside_in, beyond, nx):
    u, t, g, data, _ = refs
    nv, nt = u.shape[0], u.shape[3]
    start, wide = (2, nx + 16) if step <= 2 else (4, nx + 8)
    window = slice(start, start + wide)
    tiles = [slice(at, at + TILE) for at in range(start, start + wide, TILE)]
    right_of = lambda cols: slice(cols.start + 1, cols.stop + 1)
    keeps = {}
    for cols in tiles:
        if cols.stop > EDGE + nx:
            column = lax.broadcasted_iota(jnp.int32, (TILE, nt), 0) + cols.start
            keeps[cols.start] = jnp.logical_or(column < EDGE + nx, inside_x)
    before = {}
    last = first + count
    for low in range(first, last, CHUNK):
        high = min(low + CHUNK, last)
        rows = nv * (high - low) * wide
        block = u[:, low:high, window, :].reshape(rows, nt)
        upper = block.astype(BF16)
        lower = (block - upper.astype(F32)).astype(BF16)
        both = jnp.dot(jnp.concatenate([upper, lower], axis=1), g, preferred_element_type=F32)
        data[0:rows, :] = both[:, 0:nt] + both[:, nt : 2 * nt]
        top = lax.broadcasted_iota(jnp.int32, (TILE, nt), 0) == 0
        if low == first:
            for cols in tiles:
                a, b = t[0, first - 1, cols, :], t[1, first - 1, cols, :]
                for v in range(nv):
                    here = u[v, above, cols, :]
                    step_x = u[v, above, right_of(cols), :] - here
                    before[v, cols.start] = a * (u[v, first, cols, :] - here) + b * step_x
        for e in range(low, high):
            after = below if e == last - 1 else e + 1
            carried = [None] * nv
            for cols in tiles:
                a, b, c = t[0, e, cols, :], t[1, e, cols, :], t[2, e, cols, :]
                for v in range(nv):
                    here = u[v, e, cols, :]
                    step_in = u[v, after, cols, :] - here
                    step_x = u[v, e, right_of(cols), :] - here
                    flux_in = a * step_in + b * step_x
                    flux_x = b * step_in + c * step_x
                    turned = pltpu.roll(flux_x, 1, 0)
                    shifted = turned if carried[v] is None else jnp.where(top, carried[v], turned)
                    carried[v] = turned
                    at = (v * (high - low) + e - low) * wide + cols.start - start
                    turn = (flux_in - before[v, cols.start]) + (flux_x - shifted)
                    renewed = data[at : at + TILE, :] + turn
                    before[v, cols.start] = flux_in
                    if e >= beyond:
                        renewed = jnp.where(inside_in, renewed, 0.0)
                    if cols.start in keeps:
                        renewed = jnp.where(keeps[cols.start], renewed, 0.0)
                    u[v, e, cols, :] = renewed


TILE = 8
CHUNK = 20


def sweep_scratch(message_rows, nv, nx, nt):
    return [
        pltpu.VMEM((message_rows, nt), F32),
        pltpu.VMEM((nv * CHUNK * (nx + 16), nt), F32),
        pltpu.VMEM((CHUNK * nv, nx + 24, nt), F32),
    ]


def inner(axis):
    return lax.axis_index(axis) < lax.axis_size(axis) - 1


def sweep_far(probes, diffusion, even_x, odd_x, message, matrix):
    nv, ni, nx, nt = probes.shape
    nc = diffusion.shape[0]
    height, width = ni + 2 * STEPS, nx + 3 * EDGE

    def kernel(u0, t0, even_ref, odd_ref, message_ref, g_ref, u, t, halo_x, halo, data, cross):
        inside_x, inside_in = inner("xline"), None
        refs = (u, t, g_ref[...], data, cross)
        lay_out(u0, t0, even_ref, odd_ref, u, t, halo_x)

        def run(odd):
            take_rows(0 if odd else STEPS + ni, not odd, message_ref, halo, u, t, nx)
            for step in range(1, STEPS + 1):
                first = step if odd else STEPS + step
                count = ni + STEPS - 2 * step
                border = first + count - 1 if odd else first
                for v in range(nv):
                    u[v, height + step - 1] = u[v, border]
                advance(step, first, count, first - 1, first + count, refs, inside_x, inside_in, height, nx)

        odd = parity("inline")
        pl.when(odd == 0)(lambda: run(False))
        pl.when(odd == 1)(lambda: run(True))

    return pl.pallas_call(
        kernel,
        out_shape=(
            jax.ShapeDtypeStruct((nv, height + STEPS, width, nt), F32),
            jax.ShapeDtypeStruct((nc, height, width, nt), F32),
        ),
        in_specs=[VMEM] * 6,
        out_specs=(VMEM, VMEM),
        scratch_shapes=[pltpu.VMEM((2, even_x.shape[0], nt), F32)] + sweep_scratch(message.shape[0], nv, nx, nt),
        compiler_params=pltpu.CompilerParams(vmem_limit_bytes=8 << 20),
        cost_estimate=pl.CostEstimate(flops=1 << 28, bytes_accessed=16 << 20, transcendentals=0),
        name="sweep_far",
    )(probes, diffusion, even_x, odd_x, message, matrix)


def sweep_near(u, t, message, corners, matrix, ni, nx):
    nv, _, _, nt = u.shape
    height = ni + 2 * STEPS

    def kernel(u_in, t_in, message_ref, corners_ref, g_ref, out_hbm, u, t, halo, data, cross, sems):
        inside_x, inside_in = inner("xline"), inner("inline")
        refs = (u, t, g_ref[...], data, cross)

        def result(row, count, k):
            source = u.at[:, pl.ds(STEPS + row, count), pl.ds(EDGE, nx), :]
            return pltpu.make_async_copy(source, out_hbm.at[:, pl.ds(row, count), :, :], sems.at[k])

        def run(odd):
            ready = result(0 if odd else STEPS, ni - STEPS, 0)
            ready.start()
            take_split_rows(STEPS + ni if odd else 0, odd, message_ref, corners_ref, halo, u, t, nx)
            for step in range(1, STEPS + 1):
                first = STEPS + ni - step if odd else step
                kept = height + step - 1
                above = kept if odd else first - 1
                below = first + STEPS if odd else kept
                advance(step, first, STEPS, above, below, refs, inside_x, inside_in, STEPS + ni if odd else height, nx)
            rest = result(ni - STEPS if odd else 0, STEPS, 1)
            rest.start()
            ready.wait()
            rest.wait()

        odd = parity("inline")
        pl.when(odd == 0)(lambda: run(False))
        pl.when(odd == 1)(lambda: run(True))

    out = pl.pallas_call(
        kernel,
        out_shape=(
            jax.ShapeDtypeStruct((nv, ni, nx, nt), F32),
            jax.ShapeDtypeStruct(u.shape, F32),
            jax.ShapeDtypeStruct(t.shape, F32),
        ),
        in_specs=[VMEM] * 5,
        out_specs=(HBM, VMEM, VMEM),
        input_output_aliases={0: 1, 1: 2},
        scratch_shapes=sweep_scratch(corners.shape[0], nv, nx, nt) + [pltpu.SemaphoreType.DMA((2,))],
        compiler_params=pltpu.CompilerParams(vmem_limit_bytes=8 << 20),
        name="sweep_near",
    )(u, t, message, corners, matrix)
    return out[0]


def per_device(probes, diffusion, wavelet):
    _, ni, nx, _ = probes.shape
    even_x, odd_x, o_rows, probes, diffusion, matrix = pack_x(probes, diffusion, wavelet)
    odd_x = pairing(odd_x, "xline", 1)
    even_x = pairing(even_x, "xline", 0)
    o_rows = pairing(o_rows, "inline", 1)
    e_rows, corners = pack_z(probes, diffusion, even_x, odd_x)
    e_rows = pairing(e_rows, "inline", 0)
    corners = pairing(corners, "inline", 1)
    u, t = sweep_far(probes, diffusion, even_x, odd_x, e_rows, matrix)
    return sweep_near(u, t, o_rows, corners, matrix, ni, nx)


def solution(mesh):
    return jax.shard_map(
        per_device,
        mesh=mesh,
        in_specs=(P(None, "inline", "xline", None), P(None, "inline", "xline", None), P()),
        out_specs=P(None, "inline", "xline", None),
        check_vma=False,
    )
```

```python
import jax
import jax.numpy as jnp
from jax import lax
from jax.experimental import pallas as pl
from jax.experimental.pallas import tpu as pltpu
from jax.sharding import PartitionSpec as P

HALF = 20
STEPS = 6
NEAR = 2
F32, BF16 = jnp.float32, jnp.bfloat16
VMEM = pl.BlockSpec(memory_space=pltpu.VMEM)
HBM = pl.BlockSpec(memory_space=pltpu.HBM)


def pairing(value, axis, offset):
    count = lax.axis_size(axis)
    pairs = []
    for i in range(count):
        other = ((i + offset) ^ 1) - offset
        if 0 <= other < count:
            pairs.append((i, other))
    return lax.ppermute(value, axis, pairs)


def low_part(value):
    return value - value.astype(BF16).astype(F32)


def pieces_x(nv, nc):
    spans, start = {}, 0
    for v in range(nv):
        spans["u", v], start = start, start + STEPS
    for c in range(nc):
        spans["t", c], start = start, start + STEPS
    for v in range(nv):
        spans["low", v], start = start, start + NEAR
    return spans, start


def pieces_z(nv, nc, nx):
    wide = nx + 2 * STEPS
    spans, start = {}, 0
    for d in range(STEPS):
        for v in range(nv):
            spans["u", v, d], start = start, start + wide
        for c in range(nc):
            spans["t", c, d], start = start, start + wide
    for d in range(NEAR):
        for v in range(nv):
            spans["low", v, d], start = start, start + nx
    return spans, start


def padded(rows):
    return -(-rows // 16) * 16


def parity(axis):
    return lax.rem(lax.axis_index(axis), 2)


def put_matrix(w, line, out):
    nt = line.shape[1]
    line[...] = jnp.zeros_like(line)
    line[0:1, 0 : w.shape[1]] = w[...]
    middle = pltpu.roll(line[...], nt - HALF, 1)
    source = lax.broadcasted_iota(jnp.int32, (nt, nt), 0)
    target = lax.broadcasted_iota(jnp.int32, (nt, nt), 1)
    band = pltpu.roll(jnp.broadcast_to(middle[0:1, :], (nt, nt)), 0, 1, stride=1, stride_axis=0)
    band = jnp.where(jnp.abs(target - source) <= HALF, band, 0.0)
    full = -0.25 * lax.dot_general(band, band, (((1,), (1,)), ((), ())), precision=lax.Precision.HIGHEST)
    full = jnp.where(source == target, 1.0 + full, full)
    high = full.astype(BF16)
    out[0:nt, 0:nt] = high
    out[nt : 2 * nt, 0:nt] = high
    out[0:nt, nt : 2 * nt] = (full - high.astype(F32)).astype(BF16)
    out[nt : 2 * nt, nt : 2 * nt] = jnp.zeros((nt, nt), BF16)


def pieces_o(nv, nc):
    names = [("u", v, d) for d in range(STEPS) for v in range(nv)]
    names += [("low", v, d) for d in range(NEAR) for v in range(nv)]
    names += [("t", c, d) for c in range(nc) for d in range(STEPS)]
    return {name: k for k, name in enumerate(names)}


def pack_x(probes, diffusion, wavelet):
    nv, ni, nx, nt = probes.shape
    nc = diffusion.shape[0]
    spans, each = pieces_x(nv, nc)
    o_pieces = pieces_o(nv, nc)
    rows = ni * each

    def kernel(u_hbm, t_hbm, w_hbm, even_ref, odd_ref, o_ref, u, t, g, stage, w, line, sems):
        taps = pltpu.make_async_copy(w_hbm, w, sems.at[6])
        taps.start()
        edges, middle = [], []
        for spans_of, copies in ((((0, 8), (nx - 8, 8)), edges), (((8, nx - 16),), middle)):
            for first, count in spans_of:
                for source, target in ((u_hbm, u), (t_hbm, t)):
                    part = (slice(None), slice(None), pl.ds(first, count), slice(None))
                    sem = sems.at[len(edges) + len(middle)]
                    copies.append(pltpu.make_async_copy(source.at[part], target.at[part], sem))
        for copy in edges + middle:
            copy.start()
        taps.wait()
        put_matrix(w, line, g)
        for copy in edges:
            copy.wait()
        for side in range(2):
            first = 0 if side == 0 else nx - STEPS
            near = 0 if side == 0 else nx - NEAR
            tile = 0 if side == 0 else nx - 8
            for r in range(ni):
                base = r * each
                for v in range(nv):
                    start = base + spans["u", v]
                    stage[side, start : start + STEPS, :] = u[v, r, first : first + STEPS, :]
                    start = base + spans["low", v]
                    stage[side, start : start + NEAR, :] = low_part(u[v, r, near : near + NEAR, :])
                for c in range(nc):
                    start = base + spans["t", c]
                    edge = t[c, r, tile : tile + 8, :].astype(F32)
                    stage[side, start : start + STEPS, :] = edge[first - tile : first - tile + STEPS]
        odd = parity("xline")
        even_ref[...] = stage[1 - odd].astype(BF16)
        odd_ref[...] = stage[odd].astype(BF16)

        for copy in middle:
            copy.wait()
        odd = parity("inline")
        edge, near = odd * (ni - STEPS), odd * (STEPS - NEAR)
        for d in range(STEPS):
            for v in range(nv):
                at = o_pieces["u", v, d] * nx
                o_ref[at : at + nx, :] = u[v, edge + d].astype(BF16)
            for c in range(nc):
                at = o_pieces["t", c, d] * nx
                o_ref[at : at + nx, :] = t[c, edge + d]
        for d in range(NEAR):
            for v in range(nv):
                at = o_pieces["low", v, d] * nx
                o_ref[at : at + nx, :] = low_part(u[v, edge + near + d]).astype(BF16)

    out = jax.ShapeDtypeStruct((rows, nt), BF16)
    return pl.pallas_call(
        kernel,
        out_shape=(
            out,
            out,
            jax.ShapeDtypeStruct((len(o_pieces) * nx, nt), BF16),
            jax.ShapeDtypeStruct(probes.shape, F32),
            jax.ShapeDtypeStruct(diffusion.shape, BF16),
            jax.ShapeDtypeStruct((2 * nt, 2 * nt), BF16),
        ),
        in_specs=[HBM] * 3,
        out_specs=(VMEM,) * 6,
        scratch_shapes=[
            pltpu.VMEM((2, rows, nt), F32),
            pltpu.VMEM((1, wavelet.shape[0]), F32),
            pltpu.VMEM((8, nt), F32),
            pltpu.SemaphoreType.DMA((7,)),
        ],
        compiler_params=pltpu.CompilerParams(vmem_limit_bytes=4 << 20),
        name="pack_x",
    )(*(pltpu.with_memory_space_constraint(x, pltpu.HBM) for x in (probes, diffusion, wavelet.reshape(1, -1))))


def pack_z(probes, diffusion, even_x, odd_x):
    nv, ni, nx, nt = probes.shape
    nc = diffusion.shape[0]
    x_spans, x_each = pieces_x(nv, nc)
    spans, used = pieces_z(nv, nc, nx)
    corners, c_used = pieces_z(nv, nc, 0)
    rows, c_rows = padded(used), padded(c_used)

    def kernel(u, t, even_x_ref, odd_x_ref, e_ref, c_ref, halo, stage, stage_c):
        odd = parity("xline")
        halo[1 - odd] = even_x_ref[...].astype(F32)
        halo[odd] = odd_x_ref[...].astype(F32)
        for side in range(2):
            if rows > used:
                stage[side, used:rows, :] = jnp.zeros((rows - used, nt), F32)
            if c_rows > c_used:
                stage_c[side, c_used:c_rows, :] = jnp.zeros((c_rows - c_used, nt), F32)
            for d in range(STEPS):
                r = d if side == 0 else ni - STEPS + d
                for kind, count, ref in (("u", nv, u), ("t", nc, t)):
                    for k in range(count):
                        start = spans[kind, k, d]
                        at = r * x_each + x_spans[kind, k]
                        on_left, on_right = halo[0, at : at + STEPS, :], halo[1, at : at + STEPS, :]
                        stage[side, start : start + STEPS, :] = on_left
                        stage[side, start + STEPS : start + STEPS + nx, :] = ref[k, r, :, :].astype(F32)
                        stage[side, start + STEPS + nx : start + 2 * STEPS + nx, :] = on_right
                        start = corners[kind, k, d]
                        stage_c[side, start : start + STEPS, :] = on_left
                        stage_c[side, start + STEPS : start + 2 * STEPS, :] = on_right
            for d in range(NEAR):
                r = d if side == 0 else ni - NEAR + d
                for v in range(nv):
                    start = spans["low", v, d]
                    stage[side, start : start + nx, :] = low_part(u[v, r, :, :])
        odd = parity("inline")
        c_ref[...] = stage_c[odd].astype(BF16)
        e_ref[...] = stage[1 - odd].astype(BF16)

    return pl.pallas_call(
        kernel,
        out_shape=(jax.ShapeDtypeStruct((rows, nt), BF16), jax.ShapeDtypeStruct((c_rows, nt), BF16)),
        in_specs=[VMEM] * 4,
        out_specs=(VMEM, VMEM),
        scratch_shapes=[
            pltpu.VMEM((2, ni * x_each, nt), F32),
            pltpu.VMEM((2, rows, nt), F32),
            pltpu.VMEM((2, c_rows, nt), F32),
        ],
        compiler_params=pltpu.CompilerParams(vmem_limit_bytes=8 << 20),
        name="pack_z",
    )(probes, diffusion, even_x, odd_x)


EDGE = 8


def lay_out(u0, t0, even_ref, odd_ref, u, t, halo):
    nv, ni, nx, _ = u0.shape
    nc = t0.shape[0]
    spans, each = pieces_x(nv, nc)
    odd = parity("xline")
    halo[1 - odd] = even_ref[...].astype(F32)
    halo[odd] = odd_ref[...].astype(F32)
    for v in range(nv):
        u[v, STEPS : STEPS + ni, EDGE : EDGE + nx, :] = u0[v]
    for c in range(nc):
        t[c, STEPS : STEPS + ni, EDGE : EDGE + nx, :] = 0.25 * t0[c].astype(F32)
    for r in range(ni):
        e, base = r + STEPS, r * each
        for side, first, near in ((0, EDGE - STEPS, STEPS - NEAR), (1, EDGE + nx, 0)):
            for v in range(nv):
                at, low = base + spans["u", v], base + spans["low", v]
                u[v, e, first : first + STEPS, :] = halo[side, at : at + STEPS, :]
                u[v, e, first + near : first + near + NEAR, :] = (
                    halo[side, at + near : at + near + NEAR, :] + halo[side, low : low + NEAR, :]
                )
            for c in range(nc):
                at = base + spans["t", c]
                t[c, e, first : first + STEPS, :] = 0.25 * halo[side, at : at + STEPS, :]


def take_rows(first, high_side, message, halo, u, t, nx):
    spans, _ = pieces_z(u.shape[0], t.shape[0], nx)
    halo[...] = message[...].astype(F32)
    left, wide = EDGE - STEPS, nx + 2 * STEPS
    near = 0 if high_side else STEPS - NEAR
    for d in range(STEPS):
        for v in range(u.shape[0]):
            at = spans["u", v, d]
            u[v, first + d, left : left + wide, :] = halo[at : at + wide, :]
        for c in range(t.shape[0]):
            at = spans["t", c, d]
            t[c, first + d, left : left + wide, :] = 0.25 * halo[at : at + wide, :]
    for d in range(NEAR):
        for v in range(u.shape[0]):
            at, e = spans["low", v, d], first + near + d
            u[v, e, EDGE : EDGE + nx, :] = u[v, e, EDGE : EDGE + nx, :] + halo[at : at + nx, :]


def take_split_rows(first, high_side, rows, corners, halo, u, t, nx):
    spans, _ = pieces_z(u.shape[0], t.shape[0], 0)
    pieces = pieces_o(u.shape[0], t.shape[0])
    halo[...] = corners[...].astype(F32)
    near = 0 if high_side else STEPS - NEAR
    for d in range(STEPS):
        for kind, ref, scale in (("u", u, 1.0), ("t", t, 0.25)):
            for k in range(ref.shape[0]):
                at = spans[kind, k, d]
                ref[k, first + d, EDGE - STEPS : EDGE, :] = scale * halo[at : at + STEPS, :]
                ref[k, first + d, EDGE + nx : EDGE + nx + STEPS, :] = scale * halo[at + STEPS : at + 2 * STEPS, :]
                at = pieces[kind, k, d] * nx
                whole = rows[at : at + nx, :].astype(F32)
                if kind == "u" and near <= d < near + NEAR:
                    at = pieces["low", k, d - near] * nx
                    whole = whole + rows[at : at + nx, :].astype(F32)
                ref[k, first + d, EDGE : EDGE + nx, :] = scale * whole


def advance(step, first, count, above, below, refs, inside_x, inside_in, beyond, nx):
    u, t, g, _, _ = refs
    nv, nt = u.shape[0], u.shape[3]
    start, wide = (2, nx + 16) if step <= 2 else (4, nx + 8)
    window = slice(start, start + wide)
    tiles = [slice(at, at + TILE) for at in range(start, start + wide, TILE)]
    right_of = lambda cols: slice(cols.start + 1, cols.stop + 1)
    keeps = {}
    for cols in tiles:
        if cols.stop > EDGE + nx:
            column = lax.broadcasted_iota(jnp.int32, (TILE, nt), 0) + cols.start
            keeps[cols.start] = jnp.logical_or(column < EDGE + nx, inside_x)
    before = {}
    last = first + count
    for low in range(first, last, CHUNK):
        high = min(low + CHUNK, last)
        rows = nv * (high - low) * wide
        block = u[:, low:high, window, :].reshape(rows, nt)
        upper = block.astype(BF16)
        lower = (block - upper.astype(F32)).astype(BF16)
        both = jnp.dot(jnp.concatenate([upper, lower], axis=1), g, preferred_element_type=F32)
        top = lax.broadcasted_iota(jnp.int32, (TILE, nt), 0) == 0
        if low == first:
            for cols in tiles:
                a, b = t[0, first - 1, cols, :], t[1, first - 1, cols, :]
                for v in range(nv):
                    here = u[v, above, cols, :]
                    step_x = u[v, above, right_of(cols), :] - here
                    before[v, cols.start] = a * (u[v, first, cols, :] - here) + b * step_x
        for e in range(low, high):
            after = below if e == last - 1 else e + 1
            carried = [None] * nv
            for cols in tiles:
                a, b, c = t[0, e, cols, :], t[1, e, cols, :], t[2, e, cols, :]
                for v in range(nv):
                    here = u[v, e, cols, :]
                    step_in = u[v, after, cols, :] - here
                    step_x = u[v, e, right_of(cols), :] - here
                    flux_in = a * step_in + b * step_x
                    flux_x = b * step_in + c * step_x
                    turned = pltpu.roll(flux_x, 1, 0)
                    shifted = turned if carried[v] is None else jnp.where(top, carried[v], turned)
                    carried[v] = turned
                    at = (v * (high - low) + e - low) * wide + cols.start - start
                    turn = (flux_in - before[v, cols.start]) + (flux_x - shifted)
                    renewed = (both[at : at + TILE, 0:nt] + both[at : at + TILE, nt : 2 * nt]) + turn
                    before[v, cols.start] = flux_in
                    if e >= beyond:
                        renewed = jnp.where(inside_in, renewed, 0.0)
                    if cols.start in keeps:
                        renewed = jnp.where(keeps[cols.start], renewed, 0.0)
                    u[v, e, cols, :] = renewed


TILE = 8
CHUNK = 20


def sweep_scratch(message_rows, nv, nx, nt):
    return [
        pltpu.VMEM((message_rows, nt), F32),
        pltpu.VMEM((nv * CHUNK * (nx + 16), nt), F32),
        pltpu.VMEM((CHUNK * nv, nx + 24, nt), F32),
    ]


def inner(axis):
    return lax.axis_index(axis) < lax.axis_size(axis) - 1


def sweep_far(probes, diffusion, even_x, odd_x, message, matrix):
    nv, ni, nx, nt = probes.shape
    nc = diffusion.shape[0]
    height, width = ni + 2 * STEPS, nx + 3 * EDGE

    def kernel(u0, t0, even_ref, odd_ref, message_ref, g_ref, u, t, halo_x, halo, data, cross):
        inside_x, inside_in = inner("xline"), None
        refs = (u, t, g_ref[...], data, cross)
        lay_out(u0, t0, even_ref, odd_ref, u, t, halo_x)

        def run(odd):
            take_rows(0 if odd else STEPS + ni, not odd, message_ref, halo, u, t, nx)
            for step in range(1, STEPS + 1):
                first = step if odd else STEPS + step
                count = ni + STEPS - 2 * step
                border = first + count - 1 if odd else first
                for v in range(nv):
                    u[v, height + step - 1] = u[v, border]
                advance(step, first, count, first - 1, first + count, refs, inside_x, inside_in, height, nx)

        odd = parity("inline")
        pl.when(odd == 0)(lambda: run(False))
        pl.when(odd == 1)(lambda: run(True))

    return pl.pallas_call(
        kernel,
        out_shape=(
            jax.ShapeDtypeStruct((nv, height + STEPS, width, nt), F32),
            jax.ShapeDtypeStruct((nc, height, width, nt), F32),
        ),
        in_specs=[VMEM] * 6,
        out_specs=(VMEM, VMEM),
        scratch_shapes=[pltpu.VMEM((2, even_x.shape[0], nt), F32)] + sweep_scratch(message.shape[0], nv, nx, nt),
        compiler_params=pltpu.CompilerParams(vmem_limit_bytes=8 << 20),
        cost_estimate=pl.CostEstimate(flops=1 << 28, bytes_accessed=16 << 20, transcendentals=0),
        name="sweep_far",
    )(probes, diffusion, even_x, odd_x, message, matrix)


def sweep_near(u, t, message, corners, matrix, ni, nx):
    nv, _, _, nt = u.shape
    height = ni + 2 * STEPS

    def kernel(u_in, t_in, message_ref, corners_ref, g_ref, out_hbm, u, t, halo, data, cross, sems):
        inside_x, inside_in = inner("xline"), inner("inline")
        refs = (u, t, g_ref[...], data, cross)

        def result(row, count, k):
            source = u.at[:, pl.ds(STEPS + row, count), pl.ds(EDGE, nx), :]
            return pltpu.make_async_copy(source, out_hbm.at[:, pl.ds(row, count), :, :], sems.at[k])

        def run(odd):
            ready = result(0 if odd else STEPS, ni - STEPS, 0)
            ready.start()
            take_split_rows(STEPS + ni if odd else 0, odd, message_ref, corners_ref, halo, u, t, nx)
            for step in range(1, STEPS + 1):
                first = STEPS + ni - step if odd else step
                kept = height + step - 1
                above = kept if odd else first - 1
                below = first + STEPS if odd else kept
                advance(step, first, STEPS, above, below, refs, inside_x, inside_in, STEPS + ni if odd else height, nx)
            rest = result(ni - STEPS if odd else 0, STEPS, 1)
            rest.start()
            ready.wait()
            rest.wait()

        odd = parity("inline")
        pl.when(odd == 0)(lambda: run(False))
        pl.when(odd == 1)(lambda: run(True))

    out = pl.pallas_call(
        kernel,
        out_shape=(
            jax.ShapeDtypeStruct((nv, ni, nx, nt), F32),
            jax.ShapeDtypeStruct(u.shape, F32),
            jax.ShapeDtypeStruct(t.shape, F32),
        ),
        in_specs=[VMEM] * 5,
        out_specs=(HBM, VMEM, VMEM),
        input_output_aliases={0: 1, 1: 2},
        scratch_shapes=sweep_scratch(corners.shape[0], nv, nx, nt) + [pltpu.SemaphoreType.DMA((2,))],
        compiler_params=pltpu.CompilerParams(vmem_limit_bytes=8 << 20),
        name="sweep_near",
    )(u, t, message, corners, matrix)
    return out[0]


def per_device(probes, diffusion, wavelet):
    _, ni, nx, _ = probes.shape
    even_x, odd_x, o_rows, probes, diffusion, matrix = pack_x(probes, diffusion, wavelet)
    odd_x = pairing(odd_x, "xline", 1)
    even_x = pairing(even_x, "xline", 0)
    o_rows = pairing(o_rows, "inline", 1)
    e_rows, corners = pack_z(probes, diffusion, even_x, odd_x)
    e_rows = pairing(e_rows, "inline", 0)
    corners = pairing(corners, "inline", 1)
    u, t = sweep_far(probes, diffusion, even_x, odd_x, e_rows, matrix)
    return sweep_near(u, t, o_rows, corners, matrix, ni, nx)


def solution(mesh):
    return jax.shard_map(
        per_device,
        mesh=mesh,
        in_specs=(P(None, "inline", "xline", None), P(None, "inline", "xline", None), P()),
        out_specs=P(None, "inline", "xline", None),
        check_vma=False,
    )
```
